128 devices in a mesh: dx: 8 (over y_lo, x), dy: 16 (over y_hi, z, core).
Axes of the slice: x: 4, y: 4 (y_hi: 2, y_lo: 2; y = y_hi * 2 + y_lo), z: 4, core: 2. Of those that a mesh axis runs over, the one named last changes fastest.
Arguments:
- fine_nodes: bfloat16 [256, 256, 512], P('dx', 'dy'), may hold values from -6 to 6
- fine_edges: bfloat16 [6, 256, 256, 512], P(None, 'dx', 'dy'), may hold values from -6 to 6
- fine_links: int32 [6, 256, 256], P(None, 'dx', 'dy'), may hold values from 0 to 48
- mid_nodes: bfloat16 [64, 64, 512], P('dx', 'dy'), may hold values from -6 to 6
- mid_edges: bfloat16 [6, 64, 64, 512], P(None, 'dx', 'dy'), may hold values from -6 to 6
- mid_links: int32 [6, 64, 64], P(None, 'dx', 'dy'), may hold values from 0 to 8
- coarse_nodes: bfloat16 [16, 16, 512], replicated, may hold values from -6 to 6
- coarse_edges: bfloat16 [6, 16, 16, 512], replicated, may hold values from -6 to 6
- coarse_links: int32 [6, 16, 16], replicated, may hold values from 0 to 255
- edge_self: bfloat16 [1, 512, 1536], replicated, may hold values from -0.25 to 0.25
- edge_sender: bfloat16 [1, 512, 1536], replicated, may hold values from -0.25 to 0.25
- edge_receiver: bfloat16 [1, 512, 1536], replicated, may hold values from -0.25 to 0.25
- edge_bias: float32 [1, 1536], replicated, may hold values from -6 to 6
- edge_output: bfloat16 [1, 1536, 512], replicated, may hold values from -0.15625 to 0.15625
- edge_gain: float32 [1, 512], replicated, may hold values from 0.1 to 1.9
- edge_shift: float32 [1, 512], replicated, may hold values from -3 to 3
- node_self: bfloat16 [1, 512, 1536], replicated, may hold values from -0.25 to 0.25
- node_summed: bfloat16 [1, 512, 1536], replicated, may hold values from -0.109375 to 0.109375
- node_bias: float32 [1, 1536], replicated, may hold values from -6 to 6
- node_output: bfloat16 [1, 1536, 512], replicated, may hold values from -0.15625 to 0.15625
- node_gain: float32 [1, 512], replicated, may hold values from 0.1 to 1.9
- node_shift: float32 [1, 512], replicated, may hold values from -3 to 3
- prolongation: bfloat16 [1, 512, 512], replicated, may hold values from -0.25 to 0.25
- pooling: bfloat16 [1, 512, 512], replicated, may hold values from -0.25 to 0.25
Outputs:
- fine_out: bfloat16 [256, 256, 512], P('dx', 'dy')
- fine_edges_out: bfloat16 [6, 256, 256, 512], P(None, 'dx', 'dy')
- mid_out: bfloat16 [64, 64, 512], P('dx', 'dy')
- mid_edges_out: bfloat16 [6, 64, 64, 512], P(None, 'dx', 'dy')
- coarse_out: bfloat16 [16, 16, 512], replicated
- coarse_edges_out: bfloat16 [6, 16, 16, 512], replicated
The draws below stay inside these ranges and needn't reach their ends.
Inputs may be any that keep to these rules, and one draw needn't show every extreme that they name: `fine_links`: code q names the sender at offset (q // 7 - 3, q % 7 - 3) from the receiver. `mid_links`: code q names the sender at offset (q // 3 - 1, q % 3 - 1) from the receiver.
All inputs are finite; a program needn't handle non-finite values.
Results may differ from the reference program's by a relative error of at most 0.012.
Values may be sent and summed in bfloat16 or wider, within the bound.
No kernel may reach another device: no remote copies, remote signals or barrier semaphores. Data moves between devices by JAX's collectives and lax.ppermute only.
A program may use at most 128 MiB of HBM per device.

```python
import math
import jax
import jax.numpy as jnp
from jax import lax

D = 512
HIDDEN_SIZE = 1536
FANOUT = 6
FINE_REACH = 3
MID_REACH = 1
LAYERS = 1
NX = 256
NY = 256
MX = 64
MY = 64
CX = 16
CY = 16


def place_ends(values, rng, smallest, top_value):
    dims = values.shape
    index_at = [jax.random.randint(jax.random.fold_in(rng, axis), (), 0, dims[axis]) for axis in range(len(dims))]
    values = values.at[tuple(index_at)].set(smallest)
    longest = dims.index(max(dims))
    index_at[longest] = (index_at[longest] + 1) % dims[longest]
    return values.at[tuple(index_at)].set(top_value)


def level_of(stream_key, dims, pieces, least, largest):
    def one(dim, parts):
        steps = jax.random.uniform(jax.random.fold_in(jax.random.fold_in(stream_key, 6), dim), (parts,), jnp.float32, least / len(pieces), largest / len(pieces))
        return jnp.repeat(jnp.exp(steps), dims[dim] // parts).reshape((-1,) + (1,) * (len(dims) - dim - 1))

    factor_of = one(*pieces[0])
    for cut in pieces[1:]:
        factor_of = factor_of * one(*cut)
    return factor_of


def normal_values(own_key, dims, scale, bound, split=(), dtype=jnp.bfloat16):
    factor_of = level_of(own_key, dims, split, -0.22, 0.18) if split else 1.0
    entries = jax.random.normal(own_key, dims, jnp.float32) * scale * factor_of
    return jnp.minimum(jnp.maximum(entries, -bound), bound).astype(dtype)


def setup_inputs(seed: int = 0) -> dict:
    splits = jax.random.split(jax.random.key(seed), 25)
    return {
        "fine_nodes": normal_values(splits[0], (NX, NY, D), 1.0, 6.0, ((0, 8), (1, 16))),
        "fine_edges": normal_values(splits[1], (FANOUT, NX, NY, D), 1.0, 6.0, ((1, 8), (2, 16))),
        "fine_links": place_ends(jax.random.randint(splits[2], (FANOUT, NX, NY), 0, (2 * FINE_REACH + 1) ** 2), jax.random.fold_in(splits[2], 1), 0, ((2 * FINE_REACH + 1) ** 2) - 1).astype(jnp.int32),
        "mid_nodes": normal_values(splits[3], (MX, MY, D), 1.0, 6.0, ((0, 8), (1, 16))),
        "mid_edges": normal_values(splits[4], (FANOUT, MX, MY, D), 1.0, 6.0, ((1, 8), (2, 16))),
        "mid_links": place_ends(jax.random.randint(splits[5], (FANOUT, MX, MY), 0, (2 * MID_REACH + 1) ** 2), jax.random.fold_in(splits[5], 1), 0, ((2 * MID_REACH + 1) ** 2) - 1).astype(jnp.int32),
        "coarse_nodes": normal_values(splits[6], (CX, CY, D), 1.0, 6.0),
        "coarse_edges": normal_values(splits[7], (FANOUT, CX, CY, D), 1.0, 6.0),
        "coarse_links": place_ends(jax.random.randint(splits[8], (FANOUT, CX, CY), 0, CX * CY), jax.random.fold_in(splits[8], 1), 0, (CX * CY) - 1).astype(jnp.int32),
        "edge_self": normal_values(splits[9], (LAYERS, D, HIDDEN_SIZE), D ** -0.5, 0.25),
        "edge_sender": normal_values(splits[10], (LAYERS, D, HIDDEN_SIZE), D ** -0.5, 0.25),
        "edge_receiver": normal_values(splits[11], (LAYERS, D, HIDDEN_SIZE), D ** -0.5, 0.25),
        "edge_bias": normal_values(splits[12], (LAYERS, HIDDEN_SIZE), 1.0, 6.0, (), jnp.float32),
        "edge_output": normal_values(splits[13], (LAYERS, HIDDEN_SIZE, D), HIDDEN_SIZE ** -0.5, 0.15625),
        "edge_gain": jnp.clip(1.0 + 0.18 * jax.random.normal(splits[14], (LAYERS, D), jnp.float32), 0.1, 1.9),
        "edge_shift": normal_values(splits[15], (LAYERS, D), 0.5, 3.0, (), jnp.float32),
        "node_self": normal_values(splits[16], (LAYERS, D, HIDDEN_SIZE), D ** -0.5, 0.25),
        "node_summed": normal_values(splits[17], (LAYERS, D, HIDDEN_SIZE), (FANOUT * D) ** -0.5, 0.109375),
        "node_bias": normal_values(splits[18], (LAYERS, HIDDEN_SIZE), 1.0, 6.0, (), jnp.float32),
        "node_output": normal_values(splits[19], (LAYERS, HIDDEN_SIZE, D), HIDDEN_SIZE ** -0.5, 0.15625),
        "node_gain": jnp.clip(1.0 + 0.18 * jax.random.normal(splits[20], (LAYERS, D), jnp.float32), 0.1, 1.9),
        "node_shift": normal_values(splits[21], (LAYERS, D), 0.5, 3.0, (), jnp.float32),
        "prolongation": normal_values(splits[22], (LAYERS, D, D), D ** -0.5, 0.25),
        "pooling": normal_values(splits[23], (LAYERS, D, D), D ** -0.5, 0.25),
    }


epsilon = 1e-05

def normalize(values, gain_term, shift_term):
    average = lax.optimization_barrier(jnp.mean(values, axis=-1, keepdims=True))
    centred = values - average
    variance = lax.optimization_barrier(jnp.mean(centred * centred, axis=-1, keepdims=True))
    return centred * lax.rsqrt(variance + epsilon) * gain_term + shift_term

def level_update(nodes, edges, sender_terms, senders, weights):
    self_matrix, receiver_matrix, edge_bias, edge_output, edge_gain, edge_shift, node_self, node_summed, node_bias, node_output, node_gain, node_shift = weights
    fanout, height, breadth, feature = edges.shape
    places = height * breadth
    flat_nodes = nodes.reshape(places, feature)
    flat_edges = edges.reshape(fanout * places, feature)
    receiver = jnp.dot(flat_nodes, receiver_matrix, preferred_element_type=jnp.float32) + edge_bias
    latent = jnp.dot(flat_edges, self_matrix, preferred_element_type=jnp.float32).reshape(fanout, places, -1)
    latent = latent + jnp.take(sender_terms, senders.reshape(fanout, places), axis=0) + receiver[None]
    hidden = jax.nn.silu(latent).astype(jnp.bfloat16).reshape(fanout * places, -1)
    message = jnp.dot(hidden, edge_output, preferred_element_type=jnp.float32)
    new_edges = (flat_edges.astype(jnp.float32) + normalize(message, edge_gain, edge_shift)).astype(jnp.bfloat16)
    new_edges = new_edges.reshape(fanout, places, feature)
    summed = lax.optimization_barrier(jnp.sum(new_edges.astype(jnp.float32), axis=0)).astype(jnp.bfloat16)
    node_hidden = jnp.dot(flat_nodes, node_self, preferred_element_type=jnp.float32)
    node_hidden = node_hidden + jnp.dot(summed, node_summed, preferred_element_type=jnp.float32) + node_bias
    node_hidden = jax.nn.silu(node_hidden).astype(jnp.bfloat16)
    node_message = jnp.dot(node_hidden, node_output, preferred_element_type=jnp.float32)
    new_nodes = (flat_nodes.astype(jnp.float32) + normalize(node_message, node_gain, node_shift)).astype(jnp.bfloat16)
    return (new_nodes.reshape(height, breadth, feature), new_edges.reshape(fanout, height, breadth, feature))

def blocked_update(nodes, edges, sender_terms, senders, weights):
    height, breadth, feature = nodes.shape
    fanout = edges.shape[0]
    block = math.gcd(height, 8)
    groups = height // block
    node_blocks = nodes.reshape(groups, block, breadth, feature)
    edge_blocks = edges.reshape(fanout, groups, block, breadth, feature).transpose(1, 0, 2, 3, 4)
    index_blocks = senders.reshape(fanout, groups, block, breadth).transpose(1, 0, 2, 3)
    new_nodes, new_edges = lax.map(lambda block_items: level_update(block_items[0], block_items[1], sender_terms, block_items[2], weights), (node_blocks, edge_blocks, index_blocks))
    new_nodes = new_nodes.reshape(height, breadth, feature)
    new_edges = new_edges.transpose(1, 0, 2, 3, 4).reshape(fanout, height, breadth, feature)
    return (new_nodes, new_edges)

def offset_index(link_codes, reach_cells, padded_breadth):
    window_span = 2 * reach_cells + 1
    row_place = lax.broadcasted_iota(jnp.int32, link_codes.shape, 1)
    col_place = lax.broadcasted_iota(jnp.int32, link_codes.shape, 2)
    return ((row_place + link_codes // window_span) * padded_breadth + col_place + link_codes % window_span).astype(jnp.int32)

def widen(parent_values, height, breadth):
    parent_rows, parent_cols, feature = parent_values.shape
    spread_out = jnp.broadcast_to(parent_values[:, None, :, None, :], (parent_rows, 4, parent_cols, 4, feature))
    return spread_out.reshape(height, breadth, feature)

def reference(fine_nodes, fine_edges, fine_links, mid_nodes, mid_edges, mid_links, coarse_nodes, coarse_edges, coarse_links, edge_self, edge_sender, edge_receiver, edge_bias, edge_output, edge_gain, edge_shift, node_self, node_summed, node_bias, node_output, node_gain, node_shift, prolongation, pooling):
    fine_rows, fine_cols, feature = fine_nodes.shape
    mid_rows, mid_cols = (mid_nodes.shape[0], mid_nodes.shape[1])
    coarse_rows, coarse_cols = (coarse_nodes.shape[0], coarse_nodes.shape[1])
    for layer_index in range(edge_self.shape[0]):
        weights = tuple((stacked[layer_index] for stacked in (edge_self, edge_receiver, edge_bias, edge_output, edge_gain, edge_shift, node_self, node_summed, node_bias, node_output, node_gain, node_shift)))
        sender_matrix = edge_sender[layer_index]
        padded = jnp.pad(fine_nodes, ((FINE_REACH, FINE_REACH), (FINE_REACH, FINE_REACH), (0, 0)), mode='wrap')
        fine_terms = jnp.dot(padded.reshape(-1, feature), sender_matrix, preferred_element_type=jnp.float32)
        fine_index = offset_index(fine_links, FINE_REACH, fine_cols + 2 * FINE_REACH)
        fine_new, fine_edges = blocked_update(fine_nodes, fine_edges, fine_terms, fine_index, weights)
        pooled = mid_nodes.astype(jnp.float32).reshape(coarse_rows, 4, coarse_cols, 4, feature).mean(axis=(1, 3)).astype(jnp.bfloat16)
        raised = jnp.dot(pooled.reshape(-1, feature), pooling[layer_index], preferred_element_type=jnp.float32)
        coarse_nodes = (coarse_nodes.astype(jnp.float32) + raised.reshape(coarse_rows, coarse_cols, feature)).astype(jnp.bfloat16)
        coarse_terms = jnp.dot(coarse_nodes.reshape(-1, feature), sender_matrix, preferred_element_type=jnp.float32)
        coarse_nodes, coarse_edges = blocked_update(coarse_nodes, coarse_edges, coarse_terms, coarse_links, weights)
        lifted = jnp.dot(coarse_nodes.reshape(-1, feature), prolongation[layer_index], preferred_element_type=jnp.float32)
        lifted = lifted.reshape(coarse_rows, coarse_cols, feature)
        mid_nodes = (mid_nodes.astype(jnp.float32) + widen(lifted, mid_rows, mid_cols)).astype(jnp.bfloat16)
        padded = jnp.pad(mid_nodes, ((MID_REACH, MID_REACH), (MID_REACH, MID_REACH), (0, 0)), mode='wrap')
        mid_terms = jnp.dot(padded.reshape(-1, feature), sender_matrix, preferred_element_type=jnp.float32)
        mid_index = offset_index(mid_links, MID_REACH, mid_cols + 2 * MID_REACH)
        mid_nodes, mid_edges = blocked_update(mid_nodes, mid_edges, mid_terms, mid_index, weights)
        lifted_mid = jnp.dot(mid_nodes.reshape(-1, feature), prolongation[layer_index], preferred_element_type=jnp.float32)
        lifted_mid = lifted_mid.reshape(mid_rows, mid_cols, feature)
        fine_nodes = (fine_new.astype(jnp.float32) + widen(lifted_mid, fine_rows, fine_cols)).astype(jnp.bfloat16)
    return (fine_nodes, fine_edges, mid_nodes, mid_edges, coarse_nodes, coarse_edges)
```

```python
import functools

import jax
import jax.numpy as jnp
from jax import lax
from jax.experimental import pallas as pl
from jax.experimental.pallas import tpu as pltpu
from jax.sharding import PartitionSpec as P

EPS = 1e-05
BF = jnp.bfloat16
F32 = jnp.float32
MIB = 1 << 20


def dot(a, b):
    return jnp.dot(a, b, preferred_element_type=F32)


def onehot_rows(index_row, width):
    down = jnp.broadcast_to(index_row, (128, 128)).T
    lane = lax.broadcasted_iota(jnp.int32, (128, 128), 1)
    parts = [(down == lane + base).astype(F32).astype(BF) for base in range(0, width, 128)]
    return parts[0] if len(parts) == 1 else jnp.concatenate(parts, axis=1)


def norm(values, gain, shift):
    centred = values - jnp.mean(values, axis=-1, keepdims=True)
    variance = jnp.mean(centred * centred, axis=-1, keepdims=True)
    return centred * lax.rsqrt(variance + EPS) * gain + shift


def silu_of_half(half):
    return (half + half * jnp.tanh(half)).astype(BF)


CHUNK = 256


def sender_and_receiver(nodes_send, nodes_recv, w, table, recv):
    hidden = w.sender.shape[1]
    for n in range(0, hidden, CHUNK):
        cols = slice(n, n + CHUNK)
        table[0 : nodes_send.shape[0], cols] = (0.5 * dot(nodes_send, w.sender[:, cols])).astype(BF)
        recv[0 : nodes_recv.shape[0], cols] = 0.5 * (
            dot(nodes_recv, w.receiver[:, cols]) + w.bias[:, cols]
        )


def edge_block(edges, first_row, places, w, lhs, rhs, act, recv):
    rows, feature = edges.shape
    hidden = rhs.shape[1]
    lhs[0:rows, 0:feature] = edges
    for n in range(0, hidden, CHUNK):
        cols = slice(n, n + CHUNK)
        half = dot(lhs[0:rows, :], rhs[:, cols]).reshape(6, places, CHUNK)
        half = half + recv[pl.ds(first_row, places), cols][None]
        act[0:rows, cols] = silu_of_half(half).reshape(rows, CHUNK)
    message = dot(act[0:rows, :], w.output[...])
    new = (edges.astype(F32) + norm(message, w.gain[...], w.shift[...])).astype(BF)
    new = new.reshape(6, places, feature)
    total = new[0].astype(F32)
    for k in range(1, 6):
        total = total + new[k].astype(F32)
    return new, total.astype(BF)


def node_update(nodes, summed, w, act):
    rows = nodes.shape[0]
    hidden = w.node_self.shape[1]
    for n in range(0, hidden, CHUNK):
        cols = slice(n, n + CHUNK)
        half = 0.5 * (
            dot(nodes, w.node_self[:, cols])
            + dot(summed, w.node_summed[:, cols])
            + w.node_bias[:, cols]
        )
        act[0:rows, cols] = silu_of_half(half)
    message = dot(act[0:rows, :], w.node_output[...])
    return (nodes.astype(F32) + norm(message, w.node_gain[...], w.node_shift[...])).astype(BF)


class Weights:
    names = (
        "self", "sender", "receiver", "bias", "output", "gain", "shift",
        "node_self", "node_summed", "node_bias", "node_output", "node_gain", "node_shift",
    )

    def __init__(self, refs):
        for name, ref in zip(self.names, refs):
            setattr(self, name, ref)


COUNT = len(Weights.names)
WINDOW = 256


def load_self(w, rhs):
    rhs[0 : w.self.shape[0], :] = w.self[...] * jnp.asarray(0.5, BF)


def fine_kernel(stride, rim, nodes, index, edges, *refs):
    w = Weights(refs[:COUNT])
    new_nodes, new_edges = refs[COUNT : COUNT + 2]
    table, recv, lhs, rhs, act, summed = refs[COUNT + 2 :]
    step = pl.program_id(0)
    feature = nodes.shape[1]
    places = edges.shape[1]

    @pl.when(step == 0)
    def _():
        load_self(w, rhs)
        sender_and_receiver(rim[...], nodes[...], w, table, recv)

    for j in range(index.shape[1]):
        lhs[128 * j : 128 * j + 128, feature:] = onehot_rows(index[0, j : j + 1, :], WINDOW)
    base = pl.multiple_of(step * stride, 16)
    rhs[feature:, :] = table[pl.ds(base, WINDOW), :]
    first = pl.multiple_of(step * places, 16)
    block, total = edge_block(
        edges[...].reshape(6 * places, feature), first, places, w, lhs, rhs, act, recv
    )
    new_edges[...] = block
    summed[pl.ds(first, places), :] = total

    @pl.when(step == pl.num_programs(0) - 1)
    def _():
        new_nodes[...] = node_update(nodes[...], summed[...], w, act)


def coarse_mid_kernel(
    coarse_steps, mid_shape, coarse_shape, pooled, coarse, index, coarse_edges, mid_rim, parent, mid_index, mid_edges,
    fine, pooling, prolongation, *refs
):
    w = Weights(refs[:COUNT])
    coarse_out, coarse_edges_out, mid_out, mid_edges_out, fine_out = refs[COUNT : COUNT + 5]
    table, recv, lhs, rhs, act, summed, states = refs[COUNT + 5 :]
    step = pl.program_id(0)
    count, feature = coarse.shape
    places = coarse_edges.shape[1]

    @pl.when(step == 0)
    def _():
        load_self(w, rhs)
        block_rows, block_cols, grid_cols = coarse_shape
        place = lax.broadcasted_iota(jnp.int32, (count, count), 0)
        lane = lax.broadcasted_iota(jnp.int32, (count, count), 1)
        row, col = place // grid_cols, place % grid_cols
        device = (row // block_rows) * (grid_cols // block_cols) + col // block_cols
        source = (device * block_rows + row % block_rows) * block_cols + col % block_cols
        ordered = dot((lane == source).astype(F32).astype(BF), pooled[...]).astype(BF)
        before = coarse[...].astype(F32) + dot(ordered, pooling[...])
        states[...] = before.astype(BF)
        sender_and_receiver(states[...], states[...], w, table, recv)
        rhs[feature:, :] = table[...]

    @pl.when(step < coarse_steps)
    def _():
        for j in range(index.shape[1]):
            lhs[128 * j : 128 * j + 128, feature:] = onehot_rows(index[0, j : j + 1, :], WINDOW)
        first = pl.multiple_of(step * places, 16)
        block, total = edge_block(
            coarse_edges[...].reshape(6 * places, feature), first, places, w, lhs, rhs, act, recv
        )
        coarse_edges_out[...] = block
        summed[pl.ds(first, places), :] = total

    @pl.when(step == coarse_steps)
    def _():
        mid_rows, mid_cols = mid_shape
        mid_places = mid_rows * mid_cols
        updated = node_update(states[...], summed[...], w, act)
        coarse_out[...] = updated
        lifted = dot(
            dot(onehot_rows(parent[...], WINDOW), updated).astype(BF), prolongation[...]
        )
        rim = (mid_rim[...].astype(F32) + lifted).astype(BF)
        place = lax.broadcasted_iota(jnp.int32, (mid_places, 128), 0)
        lane = lax.broadcasted_iota(jnp.int32, (mid_places, 128), 1)
        inner = (place // mid_cols + 1) * (mid_cols + 2) + place % mid_cols + 1
        own = dot((lane == inner).astype(F32).astype(BF), rim).astype(BF)
        sender_and_receiver(rim, own, w, table, recv)
        rhs[feature : feature + 128, :] = table[0:128, :]
        rows = 6 * mid_places
        for j in range(mid_index.shape[0]):
            size = min(128, rows - 128 * j)
            hot = onehot_rows(mid_index[j : j + 1, :], WINDOW)
            lhs[128 * j : 128 * j + size, feature:] = hot[0:size]
        block, total = edge_block(mid_edges[...], 0, mid_places, w, lhs, rhs, act, recv)
        mid_edges_out[...] = block.reshape(rows, feature)
        mid_new = node_update(own, total, w, act)
        mid_out[...] = mid_new
        fine_rows = fine.shape[0]
        site = lax.broadcasted_iota(jnp.int32, (fine_rows, mid_places), 0)
        which = lax.broadcasted_iota(jnp.int32, (fine_rows, mid_places), 1)
        across = 4 * mid_cols
        over = (site // (4 * across)) * mid_cols + (site % across) // 4
        widened = dot((over == which).astype(F32).astype(BF), mid_new).astype(BF)
        fine_out[...] = (fine[...].astype(F32) + dot(widened, prolongation[...])).astype(BF)


def whole():
    return pl.BlockSpec(memory_space=pltpu.VMEM)


def run_fine(rim, nodes, index, edges, weights, stride):
    count, feature = nodes.shape
    hidden = weights[0].shape[1]
    steps = index.shape[0]
    places = count // steps
    return pl.pallas_call(
        functools.partial(fine_kernel, stride),
        grid=(steps,),
        in_specs=[
            whole(),
            whole(),
            pl.BlockSpec((1,) + index.shape[1:], lambda i: (i, 0, 0)),
            pl.BlockSpec((6, places, feature), lambda i: (0, i, 0)),
        ]
        + [whole()] * COUNT,
        out_specs=[whole(), pl.BlockSpec((6, places, feature), lambda i: (0, i, 0))],
        out_shape=[
            jax.ShapeDtypeStruct((count, feature), BF),
            jax.ShapeDtypeStruct((6, count, feature), BF),
        ],
        scratch_shapes=[
            pltpu.VMEM((rim.shape[0], hidden), BF),
            pltpu.VMEM((count, hidden), F32),
            pltpu.VMEM((6 * places, feature + WINDOW), BF),
            pltpu.VMEM((feature + WINDOW, hidden), BF),
            pltpu.VMEM((max(count, 6 * places), hidden), BF),
            pltpu.VMEM((count, feature), BF),
        ],
        compiler_params=pltpu.CompilerParams(
            dimension_semantics=("arbitrary",), vmem_limit_bytes=FINE_VMEM
        ),
        cost_estimate=pl.CostEstimate(
            flops=2 * 6 * count * (2 * feature + WINDOW) * hidden + 10 * count * feature * hidden,
            bytes_accessed=16 * MIB,
            transcendentals=7 * count * hidden,
        ),
        name="fine_level",
    )(rim, nodes, index, edges, *weights)


FINE_VMEM = 30 * MIB
COARSE_VMEM = 24 * MIB


def run_coarse_mid(
    pooled, coarse, index, coarse_edges, mid_rim, parent, mid_index, mid_edges, fine, pooling,
    prolongation, weights, mid_shape, coarse_shape
):
    count, feature = coarse.shape
    hidden = weights[0].shape[1]
    steps = index.shape[0]
    places = count // steps
    mid_places = mid_shape[0] * mid_shape[1]

    def at(i):
        return jnp.minimum(i, steps - 1)

    return pl.pallas_call(
        functools.partial(coarse_mid_kernel, steps, mid_shape, coarse_shape),
        grid=(steps + 1,),
        in_specs=[
            whole(),
            whole(),
            pl.BlockSpec((1,) + index.shape[1:], lambda i: (at(i), 0, 0)),
            pl.BlockSpec((6, places, feature), lambda i: (0, at(i), 0)),
        ]
        + [whole()] * (7 + COUNT),
        out_specs=[
            whole(),
            pl.BlockSpec((6, places, feature), lambda i: (0, at(i), 0)),
            whole(),
            whole(),
            whole(),
        ],
        out_shape=[
            jax.ShapeDtypeStruct((count, feature), BF),
            jax.ShapeDtypeStruct((6, count, feature), BF),
            jax.ShapeDtypeStruct((mid_places, feature), BF),
            jax.ShapeDtypeStruct((6 * mid_places, feature), BF),
            jax.ShapeDtypeStruct(fine.shape, BF),
        ],
        scratch_shapes=[
            pltpu.VMEM((WINDOW, hidden), BF),
            pltpu.VMEM((count, hidden), F32),
            pltpu.VMEM((6 * places, feature + WINDOW), BF),
            pltpu.VMEM((feature + WINDOW, hidden), BF),
            pltpu.VMEM((max(count, 6 * places), hidden), BF),
            pltpu.VMEM((count, feature), BF),
            pltpu.VMEM((count, feature), BF),
        ],
        compiler_params=pltpu.CompilerParams(
            dimension_semantics=("arbitrary",), vmem_limit_bytes=COARSE_VMEM
        ),
        cost_estimate=pl.CostEstimate(
            flops=2 * 6 * count * (2 * feature + WINDOW) * hidden + 10 * count * feature * hidden,
            bytes_accessed=8 * MIB,
            transcendentals=7 * count * hidden,
        ),
        name="coarse_mid_levels",
    )(
        pooled, coarse, index, coarse_edges, mid_rim, parent, mid_index, mid_edges, fine, pooling,
        prolongation, *weights
    )


def gather_coarse(pooled):
    devices = lax.axis_size("dx") * lax.axis_size("dy")
    own = pooled.reshape(-1, pooled.shape[-1])
    slots = jnp.broadcast_to(own[None], (devices,) + own.shape)
    received = lax.all_to_all(slots, ("dx", "dy"), 0, 0, tiled=True)
    return received.reshape(-1, own.shape[-1])


def per_device(
    fine_nodes, fine_edges, fine_links, mid_nodes, mid_edges, mid_links, coarse_nodes, coarse_edges,
    coarse_links, edge_self, edge_sender, edge_receiver, edge_bias, edge_output, edge_gain,
    edge_shift, node_self, node_summed, node_bias, node_output, node_gain, node_shift, prolongation,
    pooling,
):
    rows, cols, feature = fine_nodes.shape
    mid_rows, mid_cols = mid_nodes.shape[0], mid_nodes.shape[1]
    coarse_rows, coarse_cols = coarse_nodes.shape[0], coarse_nodes.shape[1]
    block_rows, block_cols = mid_rows // 4, mid_cols // 4
    weights = (
        edge_self[0], edge_sender[0], edge_receiver[0], edge_bias, edge_output[0], edge_gain,
        edge_shift, node_self[0], node_summed[0], node_bias, node_output[0], node_gain, node_shift,
    )
    pooled = (
        mid_nodes.astype(F32)
        .reshape(block_rows, 4, block_cols, 4, feature)
        .mean(axis=(1, 3))
        .astype(BF)
    )
    gathered = gather_coarse(pooled)

    def packed(fine_part, mid_part):
        return jnp.concatenate(
            [fine_part.reshape(-1, feature), mid_part.reshape(-1, feature)], axis=0
        )

    def exchange(fine, mid, axis, dim):
        count = lax.axis_size(axis)
        up = [(i, (i + 1) % count) for i in range(count)]
        down = [(j, i) for i, j in up]

        def edge(lo_fine, hi_fine, lo_mid, hi_mid):
            return (
                lax.slice_in_dim(fine, lo_fine, hi_fine, axis=dim),
                lax.slice_in_dim(mid, lo_mid, hi_mid, axis=dim),
            )

        fine_length, mid_length = fine.shape[dim], mid.shape[dim]
        last = edge(fine_length - 3, fine_length, mid_length - 1, mid_length)
        first = edge(0, 3, 0, 1)
        before = lax.ppermute(packed(*last), axis, up)
        after = lax.ppermute(packed(*first), axis, down)
        split = last[0].shape[0] * last[0].shape[1]

        def parted(rows_in):
            return rows_in[:split].reshape(last[0].shape), rows_in[split:].reshape(last[1].shape)

        (fine_before, mid_before), (fine_after, mid_after) = parted(before), parted(after)
        return (
            jnp.concatenate([fine_before, fine, fine_after], axis=dim),
            jnp.concatenate([mid_before, mid, mid_after], axis=dim),
        )

    fine_rim, mid_rim = exchange(fine_nodes, mid_nodes, "dx", 0)
    fine_rim, mid_rim = exchange(fine_rim, mid_rim, "dy", 1)
    width = 24
    fine_rim = jnp.pad(fine_rim, ((0, 0), (0, width - fine_rim.shape[1]), (0, 0)))
    fine_rim = jnp.pad(fine_rim.reshape(-1, feature), ((0, 16), (0, 0)))
    mid_rim = mid_rim.reshape(-1, feature)
    mid_rim = jnp.pad(mid_rim, ((0, 128 - mid_rim.shape[0]), (0, 0)))

    block = 4
    steps = rows // block
    r = lax.broadcasted_iota(jnp.int32, fine_links.shape, 1) % block
    c = lax.broadcasted_iota(jnp.int32, fine_links.shape, 2)
    fine_index = (r + fine_links // 7) * width + c + fine_links % 7
    fine_index = (
        fine_index.reshape(6, steps, block * cols).transpose(1, 0, 2).reshape(steps, -1, 128)
    )
    fine_new, fine_edges_new = run_fine(
        fine_rim,
        fine_nodes.reshape(-1, feature),
        fine_index,
        fine_edges.reshape(6, -1, feature),
        weights,
        block * width,
    )

    r = lax.broadcasted_iota(jnp.int32, mid_links.shape, 1)
    c = lax.broadcasted_iota(jnp.int32, mid_links.shape, 2)
    mid_index = (r + mid_links // 3) * (mid_cols + 2) + c + mid_links % 3
    mid_index = jnp.pad(mid_index.reshape(-1), (0, -mid_index.size % 128)).reshape(-1, 128)
    place = jnp.arange(128, dtype=jnp.int32)
    across = lax.axis_index("dx") * mid_rows - 1 + place // (mid_cols + 2)
    along = lax.axis_index("dy") * mid_cols - 1 + place % (mid_cols + 2)
    parent = (across % (4 * coarse_rows)) // 4 * coarse_cols + (along % (4 * coarse_cols)) // 4
    coarse_steps = 4
    coarse_index = coarse_links.reshape(6, coarse_steps, -1).transpose(1, 0, 2)
    coarse_index = coarse_index.reshape(coarse_steps, -1, 128)
    coarse_out, coarse_edges_new, mid_out, mid_edges_new, fine_out = run_coarse_mid(
        gathered,
        coarse_nodes.reshape(-1, feature),
        coarse_index,
        coarse_edges.reshape(6, -1, feature),
        mid_rim,
        parent[None],
        mid_index,
        mid_edges.reshape(-1, feature),
        fine_new,
        pooling[0],
        prolongation[0],
        weights,
        (mid_rows, mid_cols),
        (block_rows, block_cols, coarse_cols),
    )
    return (
        fine_out.reshape(fine_nodes.shape),
        fine_edges_new.reshape(fine_edges.shape),
        mid_out.reshape(mid_nodes.shape),
        mid_edges_new.reshape(mid_edges.shape),
        coarse_out.reshape(coarse_nodes.shape),
        coarse_edges_new.reshape(coarse_edges.shape),
    )


def solution(mesh):
    tile = P("dx", "dy", None)
    edge_tile = P(None, "dx", "dy", None)
    link_tile = P(None, "dx", "dy")
    in_specs = (tile, edge_tile, link_tile, tile, edge_tile, link_tile) + (P(),) * 18
    out_specs = (tile, edge_tile, tile, edge_tile, P(), P())
    return jax.shard_map(
        per_device, mesh=mesh, in_specs=in_specs, out_specs=out_specs, check_vma=False
    )
```
